32 devices in a mesh: groups: 2 (over x), tile: 16 (over z, y, core).
Axes of the slice: x: 2, y: 2, z: 4, core: 2. Of those that a mesh axis runs over, the one named last changes fastest.
Arguments:
- latent_rows: bfloat16 [4096, 256], P(('groups', 'tile')), parts along dimension 0, may hold values from -6 to 6
- line_order: int32 [128], P('groups'), parts along dimension 0, may hold values from 0 to 63, each once
- conv_weight: bfloat16 [3, 3, 3, 256, 128], replicated, may hold values from -0.078125 to 0.078125
- conv_bias: float32 [128], replicated, may hold values from -3 to 3
- blend_table: float32 [4, 8], replicated, may hold values from 0.25 to 4
- blend_ids: int32 [32], P('groups'), parts along dimension 0, may hold values from 0 to 3
Outputs:
- frames: bfloat16 [16, 32, 64, 128], P('groups', None, 'tile'), parts along dimension 0
The draws below stay inside these ranges and needn't reach their ends.
There are 2 independent parts, one for each index of `groups`. The reference program is written for one: setup_inputs(seed, part) draws one part's arguments, and reference() takes and returns one part's arrays. A program takes and returns all parts, laid end to end along the dimension named above; an argument that names none is the same for every part. Nothing has to cross between parts.
Inputs may be any that keep to these rules, and one draw needn't show every extreme that they name: line_order is a permutation of the 64 latent lines.
All inputs are finite; a program needn't handle non-finite values.
Results may differ from the reference program's by a relative error of at most 0.001.
Values may be sent and summed in bfloat16 or wider, within the bound.
A program may use at most 64 MiB of HBM per device.

```python
import math
import jax
import jax.numpy as jnp
from jax import lax

CI = 256
CO = 128
LT = 4
LH = 16
WD = 2
KINDS = 4
LINES = 64
WIDTH = 32
TILES = 16
TW = 8
OT = 8
OH = 32


def plant(values, key, least, high):
    index_at = [jax.random.randint(jax.random.fold_in(key, axis), (), 0, length) for axis, length in enumerate(values.shape)]
    widest = values.shape.index(max(values.shape))
    beside = index_at[:widest] + [(index_at[widest] + 1) % values.shape[widest]] + index_at[widest + 1:]
    return values.at[tuple(index_at)].set(least).at[tuple(beside)].set(high)


def level_of(rng, shape, split, low, high):
    level = 1.0
    for position, shards_of in split:
        steps = jax.random.uniform(jax.random.fold_in(jax.random.fold_in(rng, 6), position), (shards_of,), jnp.float32, low / len(split), high / len(split))
        level = level * jnp.repeat(jnp.exp(steps), shape[position] // shards_of).reshape((-1,) + (1,) * (len(shape) - 1 - position))
    return level


def noise(stream_key, extent, spread, limit, cuts=(), held_as=jnp.bfloat16):
    entries = jax.random.normal(stream_key, extent, jnp.float32) * spread
    if len(cuts) > 0:
        entries = level_of(stream_key, extent, cuts, -0.22, 0.18) * entries
    return jnp.clip(entries, min=-limit, max=limit).astype(held_as)


def setup_inputs(seed: int = 0, part: int = 0) -> dict:
    key_list = jax.random.split(jax.random.key(seed), 7)
    part_keys = jax.random.split(jax.random.fold_in(key_list[6], part), 7)
    return {
        "latent_rows": noise(part_keys[0], (LINES * WIDTH, CI), 1.0, 6.0, ((0, 16),)),
        "line_order": jax.random.permutation(part_keys[1], LINES).astype(jnp.int32),
        "conv_weight": noise(key_list[2], (3, 3, 3, CI, CO), (27 * CI) ** -0.5, 0.078125),
        "conv_bias": noise(key_list[3], (CO,), 0.5, 3.0, (), jnp.float32),
        "blend_table": jnp.clip(jnp.exp(jax.random.uniform(key_list[4], (KINDS, TW), jnp.float32, math.log(0.25), math.log(4.0))), 0.25, 4.0),
        "blend_ids": plant(jax.random.randint(part_keys[5], (TILES,), 0, KINDS), jax.random.fold_in(part_keys[5], 1), 0, KINDS - 1).astype(jnp.int32),
    }


def upsample(values):
    values = jnp.repeat(values, 2, axis=0)
    values = jnp.repeat(values, 2, axis=1)
    return jnp.repeat(values, 2, axis=2)


def decode_tile(window, conv_weight, conv_bias):
    upsampled = upsample(window).astype(jnp.float32)
    upsampled = jnp.concatenate([upsampled[:1], upsampled[:1], upsampled], axis=0)
    output = lax.conv_general_dilated(upsampled[None], conv_weight.astype(jnp.float32), (1, 1, 1), [(0, 0), (1, 1), (1, 1)], dimension_numbers=("NDHWC", "DHWIO", "NDHWC"), precision=lax.Precision.HIGHEST)[0]
    return jax.nn.silu(output + conv_bias)


def reference(latent_rows, line_order, conv_weight, conv_bias, blend_table, blend_ids):
    token_rows = latent_rows.reshape(LINES, WIDTH, CI)
    inverse = jnp.zeros((LINES,), jnp.int32).at[line_order].set(jnp.arange(LINES, dtype=jnp.int32))
    latent = token_rows[inverse].reshape(LT, LH, WIDTH, CI)
    padded = jnp.pad(latent, ((0, 0), (0, 0), (1, 1), (0, 0)))
    profiles = blend_table[blend_ids]

    def add_tile(totals, tile_at):
        blended, weight_sum = totals
        window = lax.dynamic_slice_in_dim(padded, tile_at * WD, WD + 2, 2)
        decoded = decode_tile(window, conv_weight, conv_bias)
        profile_row = lax.dynamic_index_in_dim(profiles, tile_at, 0, keepdims=False)
        start = (2 * WD * tile_at).astype(jnp.int32)
        current = lax.dynamic_slice_in_dim(blended, start, TW, 2)
        blended = lax.dynamic_update_slice_in_dim(blended, current + profile_row[None, None, :, None] * decoded, start, 2)
        current_sum = lax.dynamic_slice_in_dim(weight_sum, start, TW, 0)
        weight_sum = lax.dynamic_update_slice_in_dim(weight_sum, current_sum + profile_row, start, 0)
        return (blended, weight_sum), None

    start_totals = (jnp.zeros((OT, OH, 2 * WIDTH + 4, CO), jnp.float32), jnp.zeros((2 * WIDTH + 4,), jnp.float32))
    (blended, weight_sum), unused = lax.scan(add_tile, start_totals, jnp.arange(TILES, dtype=jnp.int32))
    return (blended[:, :, 2:-2] / weight_sum[2:-2][None, None, :, None]).astype(jnp.bfloat16)
```

```python
import functools

import jax
import jax.numpy as jnp
from jax import lax
from jax.experimental import pallas as pl
from jax.experimental.pallas import tpu as pltpu
from jax.sharding import PartitionSpec as P

LT = 4
WD = 2
KW = WD + 2
F32 = jnp.float32
BF16 = jnp.bfloat16
MESH = pl.DeviceIdType.MESH


def log2(n):
    assert n & (n - 1) == 0
    return n.bit_length() - 1


def iota(shape, dim):
    return lax.broadcasted_iota(jnp.int32, shape, dim)


def dot(a, b):
    return jnp.dot(a, b, preferred_element_type=F32)


def kernel(n, block, lines,
           rows_hbm, order_hbm, weight_hbm, bias_hbm, table_hbm, ids_hbm,
           out_ref,
           rows, order, weight, bias, table, ids, send, recv, spread,
           local_sem, send_sem, recv_sem):
    me = lax.axis_index("tile")
    lines_dev = lines // n
    width = WD * n
    barrier = pltpu.get_barrier_semaphore()
    for k in range(1, n):
        pl.semaphore_signal(barrier, inc=1, device_id={"tile": lax.rem(me + k, n)}, device_id_type=MESH)
    loads = [
        pltpu.make_async_copy(source, target, local_sem.at[at])
        for at, (source, target) in enumerate((
            (rows_hbm, rows), (order_hbm, order), (bias_hbm, bias),
            (table_hbm, table), (ids_hbm, ids), (weight_hbm, weight)))
    ]
    for load in loads:
        load.start()

    shape = (n * block, rows.shape[0])
    at = iota(shape, 0)
    to = at >> log2(block)
    inside = at & (block - 1)
    column = (inside >> log2(lines_dev)) + to * WD - 1
    line = inside & (lines_dev - 1)
    chosen = (iota(shape, 1) == line * width + column) & (column >= 0) & (column < width) & (inside < KW * lines_dev)
    pick = jnp.where(chosen, 1.0, 0.0).astype(BF16)
    loads[0].wait()
    send[...] = dot(pick, rows[...]).astype(BF16).reshape(send.shape)

    loads[1].wait()
    received = n * block
    shape = (lines, received)
    at = iota(shape, 1)
    inside = at & (block - 1)
    position = (at >> log2(block)) * lines_dev + (inside & (lines_dev - 1))
    expand = jnp.where(iota(shape, 0) == position, 1.0, 0.0).astype(BF16)
    held = jnp.broadcast_to(order[...].astype(F32), (8, lines)).astype(BF16)
    line_of = dot(held, expand)[:1].astype(jnp.int32)
    inside = iota((1, received), 1) & (block - 1)
    slot = jnp.where(inside < KW * lines_dev, (inside >> log2(lines_dev)) * lines + line_of, -1)
    sort = jnp.where(iota((KW * lines, received), 0) == slot, 1.0, 0.0).astype(BF16)

    pl.semaphore_wait(barrier, n - 1)
    own = pltpu.make_async_copy(send.at[me], recv.at[me], local_sem.at[6])
    own.start()

    def copy_to(k):
        peer = lax.rem(me + k, n)
        return pltpu.make_async_remote_copy(
            src_ref=send.at[peer], dst_ref=recv.at[me],
            send_sem=send_sem.at[peer], recv_sem=recv_sem.at[me],
            device_id={"tile": peer}, device_id_type=MESH)

    def copy_from(k):
        peer = lax.rem(me + k, n)
        return pltpu.make_async_remote_copy(
            src_ref=send.at[peer], dst_ref=recv.at[peer],
            send_sem=send_sem.at[peer], recv_sem=recv_sem.at[peer],
            device_id={"tile": peer}, device_id_type=MESH)

    for k in range(1, n):
        copy_to(k).start()
    for load in loads[2:]:
        load.wait()

    def profile(tile):
        kind = ids[tile]
        return [jnp.full((1, 128), table[kind, c], F32) for c in range(4 * WD)]

    has_lower = jnp.where(me > 0, 1.0, 0.0)
    has_upper = jnp.where(me < n - 1, 1.0, 0.0)
    mine = profile(me)[2:-2]
    lower = [w * has_lower for w in profile(jnp.maximum(me - 1, 0))[-2:]]
    upper = [w * has_upper for w in profile(jnp.minimum(me + 1, n - 1))[:2]]
    other = lower + upper
    total = [a + b for a, b in zip(mine, other)]
    mine = [a / t for a, t in zip(mine, total)]
    other = [b / t for b, t in zip(other, total)]

    own.wait()
    for k in range(1, n):
        copy_from(k).wait_recv()
    x = dot(sort, recv[...].reshape(received, recv.shape[2])).astype(BF16)

    high = lines // LT
    channels = weight.shape[4]

    def earlier(y):
        return jnp.concatenate([y[:, :1], y[:, :-1]], axis=1)

    stage = {}
    for kh in range(3):
        taps = []
        for kw, (first, last) in enumerate(((0, 3), (1, 3), (1, 4))):
            both = jnp.concatenate([weight[kt, kh, kw] for kt in range(3)], axis=1)
            y = dot(x[first * lines:last * lines], both)
            y = y.reshape(last - first, LT, high, 3 * channels)
            y0, y1, y2 = (y[..., kt * channels:(kt + 1) * channels] for kt in range(3))
            even = earlier(y0 + y1) + y2
            odd = earlier(y0) + (y1 + y2)
            taps.append((even, odd))
        for a in range(2):
            k0, k1, k2 = (taps[kw][a] for kw in range(3))
            lower1 = k0[1] + k1[0]
            upper2 = k1[1] + k2[1]
            stage[kh, a] = (
                k0[0] + (k1[0] + k2[0]),
                lower1, lower1 + k2[1],
                upper2, upper2 + k0[1],
                (k0[2] + k1[1]) + k2[2],
            )

    zero = jnp.zeros((LT, 1, channels), F32)
    offset = bias[...].reshape(1, 1, channels)

    def act(v):
        v = v + offset
        return v / (1.0 + jnp.exp(-v))

    row_step = 2 * WD
    for a in range(2):
        for b in range(2):
            d = []
            for at in range(6):
                z0, z1, z2 = (stage[kh, a][at] for kh in range(3))
                if b == 0:
                    v = jnp.concatenate([zero, z0[:, :-1]], axis=1) + (z1 + z2)
                else:
                    v = (z0 + z1) + jnp.concatenate([z2[:, 1:], zero], axis=1)
                d.append(act(v))
            pairs = ((d[0], d[0]), (d[2], d[1]), (d[4], d[3]), (d[5], d[5]))
            for p, (own_d, other_d) in enumerate(pairs):
                value = mine[p] * own_d + other[p] * other_d
                for f in range(LT):
                    start = ((2 * f + a) * 2 * high + b) * row_step + p
                    spread[pl.ds(start, high, stride=2 * row_step), :] = value[f]
    out_ref[...] = spread[...].astype(BF16)
    for k in range(1, n):
        copy_to(k).wait_send()


def per_device(latent_rows, line_order, conv_weight, conv_bias, blend_table, blend_ids):
    n = lax.axis_size("tile")
    lines = line_order.shape[0]
    channels = latent_rows.shape[1]
    out_channels = conv_weight.shape[-1]
    lines_dev = lines // n
    block = 16 * -(-KW * lines_dev // 16)
    out_rows = 2 * lines * 2 * 2 * WD
    any_spec = pl.BlockSpec(memory_space=pl.ANY)
    out = pl.pallas_call(
        functools.partial(kernel, n, block, lines),
        out_shape=jax.ShapeDtypeStruct((out_rows, out_channels), BF16),
        in_specs=[any_spec] * 6,
        out_specs=pl.BlockSpec(memory_space=pltpu.VMEM),
        scratch_shapes=[
            pltpu.VMEM(latent_rows.shape, BF16),
            pltpu.VMEM((1, lines), jnp.int32),
            pltpu.VMEM(conv_weight.shape, BF16),
            pltpu.VMEM((1, out_channels), F32),
            pltpu.SMEM(blend_table.shape, F32),
            pltpu.SMEM(blend_ids.shape, jnp.int32),
            pltpu.VMEM((n, block, channels), BF16),
            pltpu.VMEM((n, block, channels), BF16),
            pltpu.VMEM((out_rows, out_channels), F32),
            pltpu.SemaphoreType.DMA((7,)),
            pltpu.SemaphoreType.DMA((n,)),
            pltpu.SemaphoreType.DMA((n,)),
        ],
        compiler_params=pltpu.CompilerParams(collective_id=0, has_side_effects=True),
    )(latent_rows, line_order.reshape(1, lines), conv_weight,
      conv_bias.reshape(1, out_channels), blend_table, blend_ids)
    return out.reshape(2 * LT, 2 * (lines // LT), 2 * WD, out_channels)


def solution(mesh):
    return jax.shard_map(
        per_device,
        mesh=mesh,
        in_specs=(P(("groups", "tile"), None), P("groups"), P(), P(), P(), P("groups")),
        out_specs=P("groups", None, "tile", None),
        check_vma=False,
    )
```

```python
import functools

import jax
import jax.numpy as jnp
from jax import lax
from jax.experimental import pallas as pl
from jax.experimental.pallas import tpu as pltpu
from jax.sharding import PartitionSpec as P

LT = 4
WD = 2
KW = WD + 2
F32 = jnp.float32
BF16 = jnp.bfloat16
MESH = pl.DeviceIdType.MESH


def log2(n):
    assert n & (n - 1) == 0
    return n.bit_length() - 1


def iota(shape, dim):
    return lax.broadcasted_iota(jnp.int32, shape, dim)


def dot(a, b):
    return jnp.dot(a, b, preferred_element_type=F32)


def kernel(n, block, lines,
           rows_hbm, order_hbm, weight_hbm, bias_hbm, table_hbm, ids_hbm,
           out_ref,
           rows, order, weight, bias, table, ids, send, recv, spread,
           local_sem, send_sem, recv_sem):
    me = lax.axis_index("tile")
    lines_dev = lines // n
    width = WD * n
    barrier = pltpu.get_barrier_semaphore()
    for k in range(1, n):
        pl.semaphore_signal(barrier, inc=1, device_id={"tile": lax.rem(me + k, n)}, device_id_type=MESH)
    loads = [
        pltpu.make_async_copy(source, target, local_sem.at[at])
        for at, (source, target) in enumerate((
            (rows_hbm, rows), (order_hbm, order), (bias_hbm, bias),
            (table_hbm, table), (ids_hbm, ids), (weight_hbm, weight)))
    ]
    for load in loads:
        load.start()

    shape = (n * block, rows.shape[0])
    at = iota(shape, 0)
    to = at >> log2(block)
    inside = at & (block - 1)
    column = (inside >> log2(lines_dev)) + to * WD - 1
    line = inside & (lines_dev - 1)
    chosen = (iota(shape, 1) == line * width + column) & (column >= 0) & (column < width) & (inside < KW * lines_dev)
    pick = jnp.where(chosen, 1.0, 0.0).astype(BF16)
    loads[0].wait()
    send[...] = dot(pick, rows[...]).astype(BF16).reshape(send.shape)

    loads[1].wait()
    received = n * block
    shape = (lines, received)
    at = iota(shape, 1)
    inside = at & (block - 1)
    position = (at >> log2(block)) * lines_dev + (inside & (lines_dev - 1))
    expand = jnp.where(iota(shape, 0) == position, 1.0, 0.0).astype(BF16)
    held = jnp.broadcast_to(order[...].astype(F32), (8, lines)).astype(BF16)
    line_of = dot(held, expand)[:1].astype(jnp.int32)
    inside = iota((1, received), 1) & (block - 1)
    slot = jnp.where(inside < KW * lines_dev, (inside >> log2(lines_dev)) * lines + line_of, -1)
    sort = jnp.where(iota((KW * lines, received), 0) == slot, 1.0, 0.0).astype(BF16)

    pl.semaphore_wait(barrier, n - 1)
    own = pltpu.make_async_copy(send.at[me], recv.at[me], local_sem.at[6])
    own.start()

    def copy_to(k):
        peer = lax.rem(me + k, n)
        return pltpu.make_async_remote_copy(
            src_ref=send.at[peer], dst_ref=recv.at[me],
            send_sem=send_sem.at[peer], recv_sem=recv_sem.at[me],
            device_id={"tile": peer}, device_id_type=MESH)

    def copy_from(k):
        peer = lax.rem(me + k, n)
        return pltpu.make_async_remote_copy(
            src_ref=send.at[peer], dst_ref=recv.at[peer],
            send_sem=send_sem.at[peer], recv_sem=recv_sem.at[peer],
            device_id={"tile": peer}, device_id_type=MESH)

    for k in range(1, n):
        copy_to(k).start()
    for load in loads[2:]:
        load.wait()

    def profile(tile):
        kind = ids[tile]
        return [jnp.full((1, 128), table[kind, c], F32) for c in range(4 * WD)]

    has_lower = jnp.where(me > 0, 1.0, 0.0)
    has_upper = jnp.where(me < n - 1, 1.0, 0.0)
    mine = profile(me)[2:-2]
    lower = [w * has_lower for w in profile(jnp.maximum(me - 1, 0))[-2:]]
    upper = [w * has_upper for w in profile(jnp.minimum(me + 1, n - 1))[:2]]
    other = lower + upper
    total = [a + b for a, b in zip(mine, other)]
    mine = [a / t for a, t in zip(mine, total)]
    other = [b / t for b, t in zip(other, total)]

    own.wait()
    for k in range(1, n):
        copy_from(k).wait_recv()
    x = dot(sort, recv[...].reshape(received, recv.shape[2])).astype(BF16)

    high = lines // LT
    channels = weight.shape[4]

    def earlier(y):
        return jnp.concatenate([y[:, :1], y[:, :-1]], axis=1)

    stage = {}
    for kh in range(3):
        taps = []
        for kw, (first, last) in enumerate(((0, 3), (1, 3), (1, 4))):
            both = jnp.concatenate([weight[kt, kh, kw] for kt in range(3)], axis=1)
            y = dot(x[first * lines:last * lines], both)
            y = y.reshape(last - first, LT, high, 3 * channels)
            y0, y1, y2 = (y[..., kt * channels:(kt + 1) * channels] for kt in range(3))
            even = earlier(y0 + y1) + y2
            odd = earlier(y0) + (y1 + y2)
            taps.append((even, odd))
        for a in range(2):
            k0, k1, k2 = (taps[kw][a] for kw in range(3))
            lower1 = k0[1] + k1[0]
            upper2 = k1[1] + k2[1]
            stage[kh, a] = (
                k0[0] + (k1[0] + k2[0]),
                lower1, lower1 + k2[1],
                upper2, upper2 + k0[1],
                (k0[2] + k1[1]) + k2[2],
            )

    zero = jnp.zeros((LT, 1, channels), F32)
    offset = bias[...].reshape(1, 1, channels)

    def act(v):
        v = v + offset
        return v / (1.0 + jnp.exp(-v))

    row_step = 2 * WD
    for a in range(2):
        for b in range(2):
            d = []
            for at in range(6):
                z0, z1, z2 = (stage[kh, a][at] for kh in range(3))
                if b == 0:
                    v = jnp.concatenate([zero, z0[:, :-1]], axis=1) + (z1 + z2)
                else:
                    v = (z0 + z1) + jnp.concatenate([z2[:, 1:], zero], axis=1)
                d.append(act(v))
            pairs = ((d[0], d[0]), (d[2], d[1]), (d[4], d[3]), (d[5], d[5]))
            for p, (own_d, other_d) in enumerate(pairs):
                value = mine[p] * own_d + other[p] * other_d
                for f in range(LT):
                    start = ((2 * f + a) * 2 * high + b) * row_step + p
                    spread[pl.ds(start, high, stride=2 * row_step), :] = value[f]
    out_ref[...] = spread[...].astype(BF16)
    for k in range(1, n):
        copy_to(k).wait_send()


def per_device(latent_rows, line_order, conv_weight, conv_bias, blend_table, blend_ids):
    n = lax.axis_size("tile")
    lines = line_order.shape[0]
    channels = latent_rows.shape[1]
    out_channels = conv_weight.shape[-1]
    lines_dev = lines // n
    block = 16 * -(-KW * lines_dev // 16)
    out_rows = 2 * lines * 2 * 2 * WD
    any_spec = pl.BlockSpec(memory_space=pltpu.HBM)
    out = pl.pallas_call(
        functools.partial(kernel, n, block, lines),
        out_shape=jax.ShapeDtypeStruct((out_rows, out_channels), BF16),
        in_specs=[any_spec] * 6,
        out_specs=pl.BlockSpec(memory_space=pltpu.VMEM),
        scratch_shapes=[
            pltpu.VMEM(latent_rows.shape, BF16),
            pltpu.VMEM((1, lines), jnp.int32),
            pltpu.VMEM(conv_weight.shape, BF16),
            pltpu.VMEM((1, out_channels), F32),
            pltpu.SMEM(blend_table.shape, F32),
            pltpu.SMEM(blend_ids.shape, jnp.int32),
            pltpu.VMEM((n, block, channels), BF16),
            pltpu.VMEM((n, block, channels), BF16),
            pltpu.VMEM((out_rows, out_channels), F32),
            pltpu.SemaphoreType.DMA((7,)),
            pltpu.SemaphoreType.DMA((n,)),
            pltpu.SemaphoreType.DMA((n,)),
        ],
        compiler_params=pltpu.CompilerParams(collective_id=0, has_side_effects=True, vmem_limit_bytes=24 << 20),
    )(*(pltpu.with_memory_space_constraint(v, pltpu.HBM) for v in (
        latent_rows, line_order.reshape(1, lines), conv_weight,
        conv_bias.reshape(1, out_channels), blend_table, blend_ids)))
    return out.reshape(2 * LT, 2 * (lines // LT), 2 * WD, out_channels)


def solution(mesh):
    return jax.shard_map(
        per_device,
        mesh=mesh,
        in_specs=(P(("groups", "tile"), None), P("groups"), P(), P(), P(), P("groups")),
        out_specs=P("groups", None, "tile", None),
        check_vma=False,
    )
```

```python
import functools

import jax
import jax.numpy as jnp
from jax import lax
from jax.experimental import pallas as pl
from jax.experimental.pallas import tpu as pltpu
from jax.sharding import PartitionSpec as P

LT = 4
WD = 2
KW = WD + 2
F32 = jnp.float32
BF16 = jnp.bfloat16
MESH = pl.DeviceIdType.MESH


def log2(n):
    assert n & (n - 1) == 0
    return n.bit_length() - 1


def iota(shape, dim):
    return lax.broadcasted_iota(jnp.int32, shape, dim)


def dot(a, b):
    return jnp.dot(a, b, preferred_element_type=F32)


def kernel(n, block, lines,
           rows_hbm, order_hbm, weight_hbm, bias_hbm, table_hbm, ids_hbm,
           out_ref,
           rows, order, weight, bias, table, ids, send, recv, spread,
           local_sem, send_sem, recv_sem):
    me = lax.axis_index("tile")
    lines_dev = lines // n
    width = WD * n
    barrier = pltpu.get_barrier_semaphore()
    loads = [
        pltpu.make_async_copy(source, target, local_sem.at[at])
        for at, (source, target) in enumerate((
            (rows_hbm, rows), (order_hbm, order), (bias_hbm, bias),
            (table_hbm, table), (ids_hbm, ids), (weight_hbm, weight)))
    ]
    loads[0].start()
    for k in range(n - 1, 0, -1):
        pl.semaphore_signal(barrier, inc=1, device_id={"tile": lax.rem(me + k, n)}, device_id_type=MESH)
    for load in loads[1:]:
        load.start()

    shape = (n * block, rows.shape[0])
    at = iota(shape, 0)
    to = at >> log2(block)
    inside = at & (block - 1)
    column = (inside >> log2(lines_dev)) + to * WD - 1
    line = inside & (lines_dev - 1)
    chosen = (iota(shape, 1) == line * width + column) & (column >= 0) & (column < width) & (inside < KW * lines_dev)
    pick = jnp.where(chosen, 1.0, 0.0).astype(BF16)
    loads[0].wait()
    send[...] = dot(pick, rows[...]).astype(BF16).reshape(send.shape)

    pl.semaphore_wait(barrier, n - 1)
    own = pltpu.make_async_copy(send.at[me], recv.at[me], local_sem.at[6])
    own.start()

    def copy_to(k):
        peer = lax.rem(me + k, n)
        return pltpu.make_async_remote_copy(
            src_ref=send.at[peer], dst_ref=recv.at[me],
            send_sem=send_sem.at[peer], recv_sem=recv_sem.at[me],
            device_id={"tile": peer}, device_id_type=MESH)

    def copy_from(k):
        peer = lax.rem(me + k, n)
        return pltpu.make_async_remote_copy(
            src_ref=send.at[peer], dst_ref=recv.at[peer],
            send_sem=send_sem.at[peer], recv_sem=recv_sem.at[peer],
            device_id={"tile": peer}, device_id_type=MESH)

    for k in range(1, n):
        copy_to(k).start()
    loads[1].wait()
    received = n * block
    shape = (lines, received)
    at = iota(shape, 1)
    inside = at & (block - 1)
    position = (at >> log2(block)) * lines_dev + (inside & (lines_dev - 1))
    expand = jnp.where(iota(shape, 0) == position, 1.0, 0.0).astype(BF16)
    held = jnp.broadcast_to(order[...].astype(F32), (8, lines)).astype(BF16)
    line_of = dot(held, expand)[:1].astype(jnp.int32)
    inside = iota((1, received), 1) & (block - 1)
    slot = jnp.where(inside < KW * lines_dev, (inside >> log2(lines_dev)) * lines + line_of, -1)
    sort = jnp.where(iota((KW * lines, received), 0) == slot, 1.0, 0.0).astype(BF16)

    for load in loads[2:]:
        load.wait()

    def profile(tile):
        kind = ids[tile]
        return [jnp.full((1, 128), table[kind, c], F32) for c in range(4 * WD)]

    has_lower = jnp.where(me > 0, 1.0, 0.0)
    has_upper = jnp.where(me < n - 1, 1.0, 0.0)
    mine = profile(me)[2:-2]
    lower = [w * has_lower for w in profile(jnp.maximum(me - 1, 0))[-2:]]
    upper = [w * has_upper for w in profile(jnp.minimum(me + 1, n - 1))[:2]]
    other = lower + upper
    total = [a + b for a, b in zip(mine, other)]
    mine = [a / t for a, t in zip(mine, total)]
    other = [b / t for b, t in zip(other, total)]

    own.wait()
    for k in range(1, n):
        copy_from(k).wait_recv()
    x = dot(sort, recv[...].reshape(received, recv.shape[2])).astype(BF16)

    high = lines // LT
    channels = weight.shape[4]

    def earlier(y):
        return jnp.concatenate([y[:, :1], y[:, :-1]], axis=1)

    stage = {}
    for kh in range(3):
        taps = []
        for kw, (first, last) in enumerate(((0, 3), (1, 3), (1, 4))):
            both = jnp.concatenate([weight[kt, kh, kw] for kt in range(3)], axis=1)
            y = dot(x[first * lines:last * lines], both)
            y = y.reshape(last - first, LT, high, 3 * channels)
            y0, y1, y2 = (y[..., kt * channels:(kt + 1) * channels] for kt in range(3))
            even = earlier(y0 + y1) + y2
            odd = earlier(y0) + (y1 + y2)
            taps.append((even, odd))
        for a in range(2):
            k0, k1, k2 = (taps[kw][a] for kw in range(3))
            lower1 = k0[1] + k1[0]
            upper2 = k1[1] + k2[1]
            stage[kh, a] = (
                k0[0] + (k1[0] + k2[0]),
                lower1, lower1 + k2[1],
                upper2, upper2 + k0[1],
                (k0[2] + k1[1]) + k2[2],
            )

    zero = jnp.zeros((LT, 1, channels), F32)
    offset = bias[...].reshape(1, 1, channels)

    def act(v):
        v = v + offset
        return v / (1.0 + jnp.exp(-v))

    row_step = 2 * WD
    for a in range(2):
        for b in range(2):
            d = []
            for at in range(6):
                z0, z1, z2 = (stage[kh, a][at] for kh in range(3))
                if b == 0:
                    v = jnp.concatenate([zero, z0[:, :-1]], axis=1) + (z1 + z2)
                else:
                    v = (z0 + z1) + jnp.concatenate([z2[:, 1:], zero], axis=1)
                d.append(act(v))
            pairs = ((d[0], d[0]), (d[2], d[1]), (d[4], d[3]), (d[5], d[5]))
            for p, (own_d, other_d) in enumerate(pairs):
                value = mine[p] * own_d + other[p] * other_d
                for f in range(LT):
                    start = ((2 * f + a) * 2 * high + b) * row_step + p
                    spread[pl.ds(start, high, stride=2 * row_step), :] = value[f]
    out_ref[...] = spread[...].astype(BF16)
    for k in range(1, n):
        copy_to(k).wait_send()


def per_device(latent_rows, line_order, conv_weight, conv_bias, blend_table, blend_ids):
    n = lax.axis_size("tile")
    lines = line_order.shape[0]
    channels = latent_rows.shape[1]
    out_channels = conv_weight.shape[-1]
    lines_dev = lines // n
    block = 16 * -(-KW * lines_dev // 16)
    out_rows = 2 * lines * 2 * 2 * WD
    any_spec = pl.BlockSpec(memory_space=pltpu.HBM)
    out = pl.pallas_call(
        functools.partial(kernel, n, block, lines),
        out_shape=jax.ShapeDtypeStruct((out_rows, out_channels), BF16),
        in_specs=[any_spec] * 6,
        out_specs=pl.BlockSpec(memory_space=pltpu.VMEM),
        scratch_shapes=[
            pltpu.VMEM(latent_rows.shape, BF16),
            pltpu.VMEM((1, lines), jnp.int32),
            pltpu.VMEM(conv_weight.shape, BF16),
            pltpu.VMEM((1, out_channels), F32),
            pltpu.SMEM(blend_table.shape, F32),
            pltpu.SMEM(blend_ids.shape, jnp.int32),
            pltpu.VMEM((n, block, channels), BF16),
            pltpu.VMEM((n, block, channels), BF16),
            pltpu.VMEM((out_rows, out_channels), F32),
            pltpu.SemaphoreType.DMA((7,)),
            pltpu.SemaphoreType.DMA((n,)),
            pltpu.SemaphoreType.DMA((n,)),
        ],
        compiler_params=pltpu.CompilerParams(collective_id=0, has_side_effects=True, vmem_limit_bytes=24 << 20),
    )(*(pltpu.with_memory_space_constraint(v, pltpu.HBM) for v in (
        latent_rows, line_order.reshape(1, lines), conv_weight,
        conv_bias.reshape(1, out_channels), blend_table, blend_ids)))
    return out.reshape(2 * LT, 2 * (lines // LT), 2 * WD, out_channels)


def solution(mesh):
    return jax.shard_map(
        per_device,
        mesh=mesh,
        in_specs=(P(("groups", "tile"), None), P("groups"), P(), P(), P(), P("groups")),
        out_specs=P("groups", None, "tile", None),
        check_vma=False,
    )
```

```python
import functools

import jax
import jax.numpy as jnp
from jax import lax
from jax.experimental import pallas as pl
from jax.experimental.pallas import tpu as pltpu
from jax.sharding import PartitionSpec as P

LT = 4
WD = 2
KW = WD + 2
F32 = jnp.float32
BF16 = jnp.bfloat16
MESH = pl.DeviceIdType.MESH


def log2(n):
    assert n & (n - 1) == 0
    return n.bit_length() - 1


def iota(shape, dim):
    return lax.broadcasted_iota(jnp.int32, shape, dim)


def dot(a, b):
    return jnp.dot(a, b, preferred_element_type=F32)


def kernel(n, block, lines,
           rows_hbm, order_hbm, weight_hbm, bias_hbm, table_hbm, ids_hbm,
           out_ref,
           rows, order, weight, bias, table, ids, send, recv, spread,
           local_sem, send_sem, recv_sem):
    me = lax.axis_index("tile")
    lines_dev = lines // n
    width = WD * n
    barrier = pltpu.get_barrier_semaphore()
    loads = [
        pltpu.make_async_copy(source, target, local_sem.at[at])
        for at, (source, target) in enumerate((
            (rows_hbm, rows), (order_hbm, order), (bias_hbm, bias),
            (table_hbm, table), (ids_hbm, ids), (weight_hbm, weight)))
    ]
    loads[0].start()
    for k in range(n - 1, 0, -1):
        pl.semaphore_signal(barrier, inc=1, device_id={"tile": lax.rem(me + k, n)}, device_id_type=MESH)

    shape = (n * block, rows.shape[0])
    at = iota(shape, 0)
    to = at >> log2(block)
    inside = at & (block - 1)
    column = (inside >> log2(lines_dev)) + to * WD - 1
    line = inside & (lines_dev - 1)
    chosen = (iota(shape, 1) == line * width + column) & (column >= 0) & (column < width) & (inside < KW * lines_dev)
    pick = jnp.where(chosen, 1.0, 0.0).astype(BF16)
    loads[0].wait()
    send[...] = dot(pick, rows[...]).astype(BF16).reshape(send.shape)

    pl.semaphore_wait(barrier, n - 1)
    own = pltpu.make_async_copy(send.at[me], recv.at[me], local_sem.at[6])
    own.start()

    def copy_to(k):
        peer = lax.rem(me + k, n)
        return pltpu.make_async_remote_copy(
            src_ref=send.at[peer], dst_ref=recv.at[me],
            send_sem=send_sem.at[peer], recv_sem=recv_sem.at[me],
            device_id={"tile": peer}, device_id_type=MESH)

    def copy_from(k):
        peer = lax.rem(me + k, n)
        return pltpu.make_async_remote_copy(
            src_ref=send.at[peer], dst_ref=recv.at[peer],
            send_sem=send_sem.at[peer], recv_sem=recv_sem.at[peer],
            device_id={"tile": peer}, device_id_type=MESH)

    for k in range(1, n):
        copy_to(k).start()
    for load in loads[1:]:
        load.start()
    loads[1].wait()
    received = n * block
    shape = (lines, received)
    at = iota(shape, 1)
    inside = at & (block - 1)
    position = (at >> log2(block)) * lines_dev + (inside & (lines_dev - 1))
    expand = jnp.where(iota(shape, 0) == position, 1.0, 0.0).astype(BF16)
    held = jnp.broadcast_to(order[...].astype(F32), (8, lines)).astype(BF16)
    line_of = dot(held, expand)[:1].astype(jnp.int32)
    inside = iota((1, received), 1) & (block - 1)
    slot = jnp.where(inside < KW * lines_dev, (inside >> log2(lines_dev)) * lines + line_of, -1)
    sort = jnp.where(iota((KW * lines, received), 0) == slot, 1.0, 0.0).astype(BF16)

    for load in loads[2:]:
        load.wait()

    def profile(tile):
        kind = ids[tile]
        return [jnp.full((1, 128), table[kind, c], F32) for c in range(4 * WD)]

    has_lower = jnp.where(me > 0, 1.0, 0.0)
    has_upper = jnp.where(me < n - 1, 1.0, 0.0)
    mine = profile(me)[2:-2]
    lower = [w * has_lower for w in profile(jnp.maximum(me - 1, 0))[-2:]]
    upper = [w * has_upper for w in profile(jnp.minimum(me + 1, n - 1))[:2]]
    other = lower + upper
    total = [a + b for a, b in zip(mine, other)]
    mine = [a / t for a, t in zip(mine, total)]
    other = [b / t for b, t in zip(other, total)]

    own.wait()
    for k in range(1, n):
        copy_from(k).wait_recv()
    x = dot(sort, recv[...].reshape(received, recv.shape[2])).astype(BF16)

    high = lines // LT
    channels = weight.shape[4]

    def earlier(y):
        return jnp.concatenate([y[:, :1], y[:, :-1]], axis=1)

    stage = {}
    for kh in range(3):
        taps = []
        for kw, (first, last) in enumerate(((0, 3), (1, 3), (1, 4))):
            both = jnp.concatenate([weight[kt, kh, kw] for kt in range(3)], axis=1)
            y = dot(x[first * lines:last * lines], both)
            y = y.reshape(last - first, LT, high, 3 * channels)
            y0, y1, y2 = (y[..., kt * channels:(kt + 1) * channels] for kt in range(3))
            even = earlier(y0 + y1) + y2
            odd = earlier(y0) + (y1 + y2)
            taps.append((even, odd))
        for a in range(2):
            k0, k1, k2 = (taps[kw][a] for kw in range(3))
            lower1 = k0[1] + k1[0]
            upper2 = k1[1] + k2[1]
            stage[kh, a] = (
                k0[0] + (k1[0] + k2[0]),
                lower1, lower1 + k2[1],
                upper2, upper2 + k0[1],
                (k0[2] + k1[1]) + k2[2],
            )

    zero = jnp.zeros((LT, 1, channels), F32)
    offset = bias[...].reshape(1, 1, channels)

    def act(v):
        v = v + offset
        return v / (1.0 + jnp.exp(-v))

    row_step = 2 * WD
    for a in range(2):
        for b in range(2):
            d = []
            for at in range(6):
                z0, z1, z2 = (stage[kh, a][at] for kh in range(3))
                if b == 0:
                    v = jnp.concatenate([zero, z0[:, :-1]], axis=1) + (z1 + z2)
                else:
                    v = (z0 + z1) + jnp.concatenate([z2[:, 1:], zero], axis=1)
                d.append(act(v))
            pairs = ((d[0], d[0]), (d[2], d[1]), (d[4], d[3]), (d[5], d[5]))
            for p, (own_d, other_d) in enumerate(pairs):
                value = mine[p] * own_d + other[p] * other_d
                for f in range(LT):
                    start = ((2 * f + a) * 2 * high + b) * row_step + p
                    spread[pl.ds(start, high, stride=2 * row_step), :] = value[f]
    out_ref[...] = spread[...].astype(BF16)
    for k in range(1, n):
        copy_to(k).wait_send()


def per_device(latent_rows, line_order, conv_weight, conv_bias, blend_table, blend_ids):
    n = lax.axis_size("tile")
    lines = line_order.shape[0]
    channels = latent_rows.shape[1]
    out_channels = conv_weight.shape[-1]
    lines_dev = lines // n
    block = 16 * -(-KW * lines_dev // 16)
    out_rows = 2 * lines * 2 * 2 * WD
    any_spec = pl.BlockSpec(memory_space=pltpu.HBM)
    out = pl.pallas_call(
        functools.partial(kernel, n, block, lines),
        out_shape=jax.ShapeDtypeStruct((out_rows, out_channels), BF16),
        in_specs=[any_spec] * 6,
        out_specs=pl.BlockSpec(memory_space=pltpu.VMEM),
        scratch_shapes=[
            pltpu.VMEM(latent_rows.shape, BF16),
            pltpu.VMEM((1, lines), jnp.int32),
            pltpu.VMEM(conv_weight.shape, BF16),
            pltpu.VMEM((1, out_channels), F32),
            pltpu.SMEM(blend_table.shape, F32),
            pltpu.SMEM(blend_ids.shape, jnp.int32),
            pltpu.VMEM((n, block, channels), BF16),
            pltpu.VMEM((n, block, channels), BF16),
            pltpu.VMEM((out_rows, out_channels), F32),
            pltpu.SemaphoreType.DMA((7,)),
            pltpu.SemaphoreType.DMA((n,)),
            pltpu.SemaphoreType.DMA((n,)),
        ],
        compiler_params=pltpu.CompilerParams(collective_id=0, has_side_effects=True, vmem_limit_bytes=24 << 20),
    )(*(pltpu.with_memory_space_constraint(v, pltpu.HBM) for v in (
        latent_rows, line_order.reshape(1, lines), conv_weight,
        conv_bias.reshape(1, out_channels), blend_table, blend_ids)))
    return out.reshape(2 * LT, 2 * (lines // LT), 2 * WD, out_channels)


def solution(mesh):
    return jax.shard_map(
        per_device,
        mesh=mesh,
        in_specs=(P(("groups", "tile"), None), P("groups"), P(), P(), P(), P("groups")),
        out_specs=P("groups", None, "tile", None),
        check_vma=False,
    )
```
